32 devices in a mesh: grp: 2 (over x), seq: 16 (over z, y, core).
Axes of the slice: x: 2, y: 2, z: 4, core: 2. Of those that a mesh axis runs over, the one named last changes fastest.
Arguments:
- conv_input: bfloat16 [8192, 4352], P(('grp', 'seq')), parts along dimension 0, may hold values from -6 to 6, as said below
- conv_weight: float32 [4, 4352], replicated, may hold values from -3 to 3
- step_logit: float32 [8192, 32], P(('grp', 'seq')), parts along dimension 0, may hold values from -20 to 0, as said below
- decay_log: float32 [32], replicated, may hold values from -0.5 to 0.5
- skip_gain: float32 [32], replicated, may hold values from 0.5 to 2
Outputs:
- mixer_out: bfloat16 [8192, 4096], P(('grp', 'seq')), parts along dimension 0
The draws below stay inside these ranges and needn't reach their ends.
There are 2 independent parts, one for each index of `grp`. The reference program is written for one: setup_inputs(seed, part) draws one part's arguments, and reference() takes and returns one part's arrays. A program takes and returns all parts, laid end to end along the dimension named above; an argument that names none is the same for every part. Nothing has to cross between parts.
Inputs may be any that keep to these rules, and one draw needn't show every extreme that they name: `conv_input`: activations before the convolution. `step_logit`: step sizes before softplus.
All inputs are finite; a program needn't handle non-finite values.
Results may differ from the reference program's by a relative error of at most 0.0047.
Values may be sent and summed in bfloat16 or wider, within the bound.
A program may use at most 128 MiB of HBM per device.

```python
import math
import jax
import jax.numpy as jnp
from jax import lax

LOCAL_HEADS = 32
HEADDIM = 128
STATE = 128
GROUP = 256
TAPS = 4
TOK_DEV = 256
CHANNELS = 4352
TOKENS = 4096


def segment_rows(key):
    return jax.random.randint(jax.random.fold_in(key, 11), (2,), 0, TOKENS)


def draw_conv_input(key, part):
    segment_list = segment_rows(key)
    base = jax.random.normal(jax.random.fold_in(key, 1), (TOKENS, CHANNELS), jnp.float32)
    column = jnp.arange(CHANNELS)[None, :]
    column_scale = jnp.where(column < LOCAL_HEADS * HEADDIM, 1.0, 0.6)
    row_offset_index = jnp.arange(TOKENS)[:, None]
    quiet = jnp.zeros((TOKENS, 1), jnp.bool_)
    for segment_index in range(2):
        token_position = segment_list[segment_index]
        quiet = quiet | (row_offset_index <= token_position) & (row_offset_index > token_position - TAPS)
    value = jnp.clip(base * column_scale, -6.0, 6.0)
    return jnp.where(quiet, 0.0, value).astype(jnp.bfloat16)


def draw_step_logit(key, part):
    segment_list = segment_rows(key)
    share_fast = 0.5
    fast_heads = jax.random.uniform(jax.random.fold_in(key, 3), (LOCAL_HEADS,), jnp.float32) < share_fast
    fast_rate = jnp.exp(jax.random.uniform(jax.random.fold_in(key, 4), (LOCAL_HEADS,), jnp.float32, math.log(1.0 / 50.0), math.log(1.0 / 30.0)))
    slow_rate = jax.random.uniform(jax.random.fold_in(key, 5), (LOCAL_HEADS,), jnp.float32, 0.1, 0.25) / GROUP
    head_rate = jnp.where(fast_heads, fast_rate, slow_rate)
    block_shift = jax.random.uniform(jax.random.fold_in(key, 6), (TOKENS // TOK_DEV, LOCAL_HEADS), jnp.float32, -0.7, 0.7)
    block_shift = jnp.repeat(block_shift, TOK_DEV, axis=0)
    rough = jax.random.uniform(jax.random.fold_in(key, 7), (TOKENS, LOCAL_HEADS), jnp.float32, -0.5, 0.5)
    time_step_size = head_rate[None, :] * jnp.exp(block_shift + rough)
    segment_decay_loss = jax.random.uniform(jax.random.fold_in(key, 8), (2, LOCAL_HEADS), jnp.float32, 0.2, 0.4)
    row_offset_index = jnp.arange(TOKENS)[:, None]
    for segment_index in range(2):
        time_step_size = jnp.where(row_offset_index == segment_list[segment_index], segment_decay_loss[segment_index][None, :], time_step_size)
    return jnp.log(-jnp.expm1(-time_step_size)) + time_step_size


def gaussian(stream_key, shape, scale, reach, kind=jnp.bfloat16):
    return jnp.clip(scale * jax.random.normal(stream_key, shape, jnp.float32), -reach, reach).astype(kind)


def setup_inputs(seed: int = 0, part: int = 0) -> dict:
    key_of = jax.random.split(jax.random.key(seed), 6)
    own_keys = jax.random.split(jax.random.fold_in(key_of[5], part), 6)
    return {
        "conv_input": draw_conv_input(jax.random.fold_in(jax.random.fold_in(key_of[5], part), 71), part),
        "conv_weight": gaussian(key_of[1], (TAPS, CHANNELS), TAPS ** -0.5, 3.0, jnp.float32),
        "step_logit": draw_step_logit(jax.random.fold_in(jax.random.fold_in(key_of[5], part), 71), part),
        "decay_log": jnp.clip(jax.random.uniform(key_of[3], (LOCAL_HEADS,), jnp.float32, -0.5, 0.5), -0.5, 0.5),
        "skip_gain": jnp.clip(jnp.exp(jax.random.uniform(key_of[4], (LOCAL_HEADS,), jnp.float32, math.log(0.5), math.log(2.0))), 0.5, 2.0),
    }


def conv_activate(extended, kernel, row_count):
    running = kernel[0] * extended[0:row_count].astype(jnp.float32)
    for tap_index in range(1, kernel.shape[0]):
        running = running + kernel[tap_index] * extended[tap_index:tap_index + row_count].astype(jnp.float32)
    return jax.nn.silu(running).astype(jnp.bfloat16)


def group_terms(activated, logits, decay_rate, skip_gain):
    head_count = decay_rate.shape[0]
    inner_width = head_count * HEADDIM
    block_count = activated.shape[0]
    span_rows = activated.shape[1]
    values = activated[:, :, :inner_width].reshape(block_count, span_rows, head_count, HEADDIM)
    b_rows = activated[:, :, inner_width:inner_width + STATE]
    c_rows = activated[:, :, inner_width + STATE:]
    time_step_size = jax.nn.softplus(logits)
    cum_decay = jnp.cumsum(time_step_size * decay_rate, axis=1)
    decay_t = jnp.transpose(cum_decay, (0, 2, 1))
    step_t = jnp.transpose(time_step_size, (0, 2, 1))
    scores = jnp.einsum('cqn,csn->cqs', c_rows.astype(jnp.float32), b_rows.astype(jnp.float32))
    token_position = jnp.arange(span_rows)
    causal = token_position[:, None] >= token_position[None, :]
    decay_gap = jnp.where(causal, decay_t[:, :, :, None] - decay_t[:, :, None, :], -jnp.inf)
    weights = (scores[:, None] * jnp.exp(decay_gap) * step_t[:, :, None, :]).astype(jnp.bfloat16)
    intra_out = jnp.einsum('chqs,cshp->cqhp', weights.astype(jnp.float32), values.astype(jnp.float32))
    local_out = intra_out + skip_gain[:, None] * values.astype(jnp.float32)
    tail_weight = jnp.transpose(jnp.exp(decay_t[:, :, -1:] - decay_t) * step_t, (0, 2, 1))
    weighted = (values.astype(jnp.float32) * tail_weight[..., None]).astype(jnp.bfloat16)
    states = jnp.einsum('cshp,csn->chpn', weighted.astype(jnp.float32), b_rows.astype(jnp.float32))
    return local_out, states, cum_decay, c_rows


def reference(conv_input, conv_weight, step_logit, decay_log, skip_gain):
    tap_count = conv_weight.shape[0]
    head_count = decay_log.shape[0]
    padded = jnp.concatenate([jnp.zeros((tap_count - 1, conv_input.shape[1]), jnp.bfloat16), conv_input], 0)
    decay_rate = -jnp.exp(decay_log)

    def group_step(current, group_index):
        start_row = (group_index * GROUP).astype(jnp.int32)
        window = lax.dynamic_slice_in_dim(padded, start_row, GROUP + tap_count - 1, 0)
        logits = lax.dynamic_slice_in_dim(step_logit, start_row, GROUP, 0)
        activated = conv_activate(window, conv_weight, GROUP)
        local_out, states, cum_decay, c_rows = group_terms(activated[None], logits[None], decay_rate, skip_gain)
        inter_out = jnp.exp(cum_decay)[..., None] * jnp.einsum('cqn,hpn->cqhp', c_rows.astype(jnp.float32), current, precision=lax.Precision.HIGHEST)
        result = (local_out + inter_out).reshape(GROUP, head_count * HEADDIM).astype(jnp.bfloat16)
        following = jnp.exp(cum_decay[0, -1])[:, None, None] * current + states[0]
        return following, result

    initial = jnp.zeros((head_count, HEADDIM, STATE), jnp.float32)
    _, blocks = lax.scan(group_step, initial, jnp.arange(TOKENS // GROUP, dtype=jnp.int32))
    return blocks.reshape(TOKENS, head_count * HEADDIM)
```

```python
import functools

import jax
import jax.numpy as jnp
from jax import lax
from jax.experimental import pallas as pl
from jax.experimental.pallas import tpu as pltpu
from jax.sharding import PartitionSpec as P

HEADDIM = 128
STATE = 128
PAIR = 2 * HEADDIM
MESH = pl.DeviceIdType.MESH
F32 = jnp.float32
BF16 = jnp.bfloat16


def softplus(x):
    e = jnp.exp(-jnp.abs(x))
    series = e * (1.0 - e * (1 / 2 - e * (1 / 3 - e * (1 / 4 - e * (1 / 5 - e * (1 / 6))))))
    return jnp.maximum(x, 0.0) + jnp.where(e < 0.03, series, jnp.log(1.0 + e))


def kernel(
    n_seq, heads, rows, taps,
    x_ref, w_ref, sl_ref, dl_ref, skip_ref, out_ref,
    halo, ext, act, b_t, c_act, scores, tail_tab, cum_tab, rowg, tot,
    s_send, s_own, s_recv, t_own, t_send, t_recv, p_send, p_recv, e_send, e_recv, ent, local,
    halo_sems, tot_sems, s_sems, t_sems, p_sems, e_sems,
):
    me = lax.axis_index("seq")
    grp = lax.axis_index("grp")
    core = me % 2
    side = (me // 2) % 2
    quad = me // 4
    quads = n_seq // 4
    place = me % 4
    half = heads // 4
    inner = heads * HEADDIM
    has_next = quad < quads - 1
    has_prev = quad > 0

    def xor_peer(r):
        flip_core = (1 - 2 * core) * (r % 2)
        flip_side = (1 - 2 * side) * (r // 2) * 2
        return me + flip_core + flip_side

    def dev(seq_index):
        return (grp, seq_index)

    barrier = pltpu.get_barrier_semaphore()
    for r in (1, 2, 3):
        pl.semaphore_signal(barrier, inc=1, device_id=dev(xor_peer(r)), device_id_type=MESH)

    @pl.when(has_next)
    def _():
        pl.semaphore_signal(barrier, inc=1, device_id=dev(me + 4), device_id_type=MESH)

        @pl.when(place == 3)
        def _():
            pl.semaphore_signal(barrier, inc=1, device_id=dev(me + 1), device_id_type=MESH)

    @pl.when(has_prev)
    def _():
        pl.semaphore_signal(barrier, inc=1, device_id=dev(me - 4), device_id_type=MESH)

        @pl.when(place == 0)
        def _():
            pl.semaphore_signal(barrier, inc=1, device_id=dev(me - 1), device_id_type=MESH)

    next_count = 1 - (quad + 1) // quads
    prev_count = (quad + quads - 1) // quads
    pl.semaphore_wait(
        barrier,
        3 + next_count * (1 + place // 3) + prev_count * (2 - (place + 3) // 4),
    )

    def remote(src, dst, sems, j, target):
        return pltpu.make_async_remote_copy(
            src_ref=src, dst_ref=dst, send_sem=sems.at[0, j], recv_sem=sems.at[1, j],
            device_id=dev(target), device_id_type=MESH,
        )

    def halo_copy():
        return remote(x_ref.at[pl.ds(rows - 16, 16)], halo, halo_sems, 0, me + 1)

    @pl.when(me < n_seq - 1)
    def _():
        halo_copy().start()

    step = softplus(sl_ref[...])
    eye = lax.broadcasted_iota(jnp.int32, (heads, heads), 0) == lax.broadcasted_iota(
        jnp.int32, (heads, heads), 1
    )
    rate = jnp.sum(jnp.where(eye, -jnp.exp(dl_ref[...]), 0.0), axis=1, keepdims=True)
    row_id = lax.broadcasted_iota(jnp.int32, (rows, rows), 0)
    col_id = lax.broadcasted_iota(jnp.int32, (rows, rows), 1)
    upto = (row_id <= col_id).astype(F32)
    cum_t = jnp.dot(
        step * rate, upto, preferred_element_type=F32, precision=lax.Precision.HIGHEST
    )
    cum_end = cum_t[:, rows - 1 : rows]
    for h in range(heads):
        tot[0, h // 2 : h // 2 + 1, pl.ds((h % 2) * HEADDIM, HEADDIM)] = jnp.broadcast_to(
            cum_end[h : h + 1, :], (1, HEADDIM)
        )
    for r in (1, 2, 3):
        remote(tot.at[0], tot.at[r], tot_sems, r, xor_peer(r)).start()
    rowg[...] = cum_t - jnp.log(step)
    cum = jnp.transpose(cum_t)
    tail = jnp.transpose(jnp.exp(cum_end - cum_t) * step)
    for h in range(heads):
        tail_tab[h] = jnp.broadcast_to(tail[:, h : h + 1], (rows, HEADDIM))
        cum_tab[h] = jnp.broadcast_to(cum[:, h : h + 1], (rows, HEADDIM))

    @pl.when(me == 0)
    def _():
        halo[...] = jnp.zeros_like(halo)

    @pl.when(me > 0)
    def _():
        halo_copy().wait_recv()

    def conv(start, slot):
        cols = pl.ds(start, PAIR)
        ext[slot, 0:8, :] = halo[:, cols].astype(F32)[8:16]
        ext[slot, 8 : 8 + rows, :] = x_ref[:, cols].astype(F32)
        total = w_ref[0:1, cols] * ext[slot, pl.ds(9 - taps, rows), :]
        for k in range(1, taps):
            total = total + w_ref[k : k + 1, cols] * ext[slot, pl.ds(9 - taps + k, rows), :]
        half_v = 0.5 * total
        return (half_v + half_v * jnp.tanh(half_v)).astype(BF16)

    maps = conv(inner, 0)
    b_rows = maps[:, :STATE]
    c_rows = maps[:, STATE:]
    b_trans = jnp.transpose(b_rows.astype(F32)).astype(BF16)
    b_t[...] = b_trans
    c_act[...] = c_rows
    raw = jnp.dot(c_rows, b_trans, preferred_element_type=F32)
    scores[...] = jnp.where(row_id >= col_id, raw, 0.0)

    own_first = half * core
    other_first = half * (1 - core)

    def pair_state(i, slot):
        a = conv(pl.multiple_of(i * PAIR, PAIR), slot)
        act[i] = a
        left = a[:, :HEADDIM].astype(F32) * tail_tab[2 * i]
        right = a[:, HEADDIM:].astype(F32) * tail_tab[2 * i + 1]
        weighted = jnp.concatenate([left.astype(BF16), right.astype(BF16)], axis=1)
        return jnp.dot(b_t[...], weighted, preferred_element_type=F32)

    def s_copy(j):
        return remote(s_send.at[j], s_recv.at[j], s_sems, j, xor_peer(1))

    def t_copy(j):
        return remote(t_send.at[j], t_recv.at[j], t_sems, j, xor_peer(2))

    def p_copy(j):
        return remote(p_send.at[j], p_recv.at[j], p_sems, j, me + 4)

    def e_copy(j):
        return remote(e_send.at[j], e_recv.at[j], e_sems, j, xor_peer(1))

    def logs(r, j):
        return tot[r, pl.ds(own_first + j, 1), :]

    def first_state(j):
        return jnp.where(core == 0, s_own[j], s_recv[j].astype(F32))

    def chip_step(j):
        s_copy(j).wait_recv()
        mine, got = s_own[j], s_recv[j].astype(F32)
        decay_last = jnp.exp(jnp.where(core == 0, logs(1, j), logs(0, j)))
        total = decay_last * jnp.where(core == 0, mine, got) + jnp.where(core == 0, got, mine)
        t_own[j] = total
        t_send[j] = total.astype(BF16)
        t_copy(j).start()

    for r in (1, 2, 3):
        remote(tot.at[0], tot.at[r], tot_sems, r, xor_peer(r)).wait_recv()

    @pl.loop(0, half)
    def _(j):
        s_send[j] = pair_state(other_first + j, 0).astype(BF16)
        s_copy(j).start()
        s_own[j] = pair_state(own_first + j, 1)

        @pl.when(j >= 1)
        def _():
            chip_step(j - 1)

    chip_step(half - 1)

    def quad_step(j):
        t_copy(j).wait_recv()
        mine, got = t_own[j], t_recv[j].astype(F32)
        log_mine = logs(0, j) + logs(1, j)
        log_got = logs(2, j) + logs(3, j)
        log_0 = jnp.where(side == 0, log_mine, log_got)
        log_1 = jnp.where(side == 0, log_got, log_mine)
        t_0 = jnp.where(side == 0, mine, got)
        t_1 = jnp.where(side == 0, got, mine)
        plane = jnp.exp(log_1) * t_0 + t_1

        @pl.when(has_prev)
        def _():
            p_copy(j).wait_recv()

        @pl.when(quad == 0)
        def _():
            p_recv[j] = jnp.zeros((STATE, PAIR), BF16)

        before = p_recv[j].astype(F32)

        @pl.when(has_next)
        def _():
            p_send[j] = (jnp.exp(log_0 + log_1) * before + plane).astype(BF16)
            p_copy(j).start()

        e_chip = jnp.where(side == 0, before, jnp.exp(log_0) * before + t_0)
        decay_first = jnp.exp(jnp.where(core == 0, logs(0, j), logs(1, j)))
        e_second = decay_first * e_chip + first_state(j)
        e_send[j] = jnp.where(core == 0, e_second, e_chip).astype(BF16)
        e_copy(j).start()
        ent[j] = jnp.where(core == 0, e_chip, e_second).astype(BF16)

    mid = rows // 2

    def intra(i):
        for u in range(2):
            h = 2 * i + u
            lanes = pl.ds(u * HEADDIM, HEADDIM)
            g = rowg[pl.ds(h, 1), :]
            col = cum_tab[h]
            v = act[i, :, lanes]
            gain = skip_ref[h]
            top = scores[0:mid, 0:mid] * jnp.exp(jnp.minimum(col[:mid] - g[:, :mid], 0.0))
            low_a = scores[mid:, 0:mid] * jnp.exp(jnp.minimum(col[mid:] - g[:, :mid], 0.0))
            low_b = scores[mid:, mid:] * jnp.exp(jnp.minimum(col[mid:] - g[:, mid:], 0.0))
            low = jnp.concatenate([low_a.astype(BF16), low_b.astype(BF16)], axis=1)
            y_top = jnp.dot(top.astype(BF16), v[:mid], preferred_element_type=F32)
            y_low = jnp.dot(low, v, preferred_element_type=F32)
            local[i, 0:mid, lanes] = y_top + gain * v[:mid].astype(F32)
            local[i, mid:, lanes] = y_low + gain * v[mid:].astype(F32)

    def finish(i, state):
        inter = jnp.dot(c_act[...], state, preferred_element_type=F32)
        grow = jnp.concatenate([jnp.exp(cum_tab[2 * i]), jnp.exp(cum_tab[2 * i + 1])], axis=1)
        out_ref[:, pl.ds(pl.multiple_of(i * PAIR, PAIR), PAIR)] = (
            local[i] + grow * inter
        ).astype(out_ref.dtype)

    def finish_step(j):
        finish(own_first + j, ent[j])
        e_copy(j).wait_recv()
        finish(other_first + j, e_recv[j])

    @pl.loop(0, half)
    def _(j):
        quad_step(j)
        intra(own_first + j)
        intra(other_first + j)

        @pl.when(j >= 1)
        def _():
            finish_step(j - 1)

    finish_step(half - 1)

    @pl.when(me < n_seq - 1)
    def _():
        halo_copy().wait_send()

    for r in (1, 2, 3):
        remote(tot.at[0], tot.at[r], tot_sems, r, xor_peer(r)).wait_send()

    @pl.loop(0, half)
    def _(j):
        s_copy(j).wait_send()
        t_copy(j).wait_send()
        e_copy(j).wait_send()

        @pl.when(has_next)
        def _():
            p_copy(j).wait_send()


def on_device(n_seq, conv_input, conv_weight, step_logit, decay_log, skip_gain):
    taps, channels = conv_weight.shape
    rows = conv_input.shape[0]
    heads = decay_log.shape[0]
    half = heads // 4
    vmem = pl.BlockSpec(memory_space=pltpu.VMEM)
    chunk = (half, STATE, PAIR)

    def pair_sems(count):
        return pltpu.SemaphoreType.DMA((2, count))

    return pl.pallas_call(
        functools.partial(kernel, n_seq, heads, rows, taps),
        out_shape=jax.ShapeDtypeStruct((rows, heads * HEADDIM), BF16),
        in_specs=[vmem, vmem, vmem, vmem, pl.BlockSpec(memory_space=pltpu.SMEM)],
        out_specs=vmem,
        scratch_shapes=[
            pltpu.VMEM((16, channels), BF16),
            pltpu.VMEM((2, rows + 8, PAIR), F32),
            pltpu.VMEM((heads // 2, rows, PAIR), BF16),
            pltpu.VMEM((STATE, rows), BF16),
            pltpu.VMEM((rows, STATE), BF16),
            pltpu.VMEM((rows, rows), F32),
            pltpu.VMEM((heads, rows, HEADDIM), F32),
            pltpu.VMEM((heads, rows, HEADDIM), F32),
            pltpu.VMEM((heads, rows), F32),
            pltpu.VMEM((4, heads // 2, PAIR), F32),
            pltpu.VMEM(chunk, BF16),
            pltpu.VMEM(chunk, F32),
            pltpu.VMEM(chunk, BF16),
            pltpu.VMEM(chunk, F32),
            pltpu.VMEM(chunk, BF16),
            pltpu.VMEM(chunk, BF16),
            pltpu.VMEM(chunk, BF16),
            pltpu.VMEM(chunk, BF16),
            pltpu.VMEM(chunk, BF16),
            pltpu.VMEM(chunk, BF16),
            pltpu.VMEM(chunk, BF16),
            pltpu.VMEM((heads // 2, rows, PAIR), F32),
            pair_sems(1),
            pair_sems(4),
            pair_sems(half),
            pair_sems(half),
            pair_sems(half),
            pair_sems(half),
        ],
        compiler_params=pltpu.CompilerParams(
            collective_id=0, has_side_effects=True, vmem_limit_bytes=48 * 1024 * 1024
        ),
    )(conv_input, conv_weight, step_logit.T, decay_log.reshape(1, heads), skip_gain)


def solution(mesh):
    return jax.shard_map(
        functools.partial(on_device, mesh.shape["seq"]),
        mesh=mesh,
        in_specs=(P(("grp", "seq"), None), P(), P(("grp", "seq"), None), P(), P()),
        out_specs=P(("grp", "seq"), None),
        check_vma=False,
    )
```

```python
import functools

import jax
import jax.numpy as jnp
from jax import lax
from jax.experimental import pallas as pl
from jax.experimental.pallas import tpu as pltpu
from jax.sharding import PartitionSpec as P

HEADDIM = 128
STATE = 128
PAIR = 2 * HEADDIM
MESH = pl.DeviceIdType.MESH
F32 = jnp.float32
BF16 = jnp.bfloat16


def softplus(x):
    e = jnp.exp(-jnp.abs(x))
    series = e * (1.0 - e * (1 / 2 - e * (1 / 3 - e * (1 / 4 - e * (1 / 5 - e * (1 / 6))))))
    return jnp.maximum(x, 0.0) + jnp.where(e < 0.03, series, jnp.log(1.0 + e))


def kernel(
    n_seq, heads, rows, taps,
    x_hbm, w_hbm, sl_hbm, dl_hbm, skip_hbm, out_ref,
    x_ref, w_ref, sl_ref, dl_ref, skip_ref, load_sems,
    gains, halo, ext, act, b_t, c_act, scores, tail_tab, cum_tab, rowg, tot,
    s_send, s_own, s_recv, t_own, t_send, t_recv, p_send, p_recv, e_send, e_recv, ent, local,
    halo_sems, tot_sems, s_sems, t_sems, p_sems, e_sems,
):
    me = lax.axis_index("seq")
    grp = lax.axis_index("grp")
    core = me % 2
    side = (me // 2) % 2
    quad = me // 4
    quads = n_seq // 4
    place = me % 4
    half = heads // 4
    inner = heads * HEADDIM
    has_next = quad < quads - 1
    has_prev = quad > 0

    def xor_peer(r):
        flip_core = (1 - 2 * core) * (r % 2)
        flip_side = (1 - 2 * side) * (r // 2) * 2
        return me + flip_core + flip_side

    def dev(seq_index):
        return (grp, seq_index)

    loads = [
        pltpu.make_async_copy(source, target, load_sems.at[k])
        for k, (source, target) in enumerate(
            (
                (sl_hbm, sl_ref),
                (dl_hbm, dl_ref),
                (skip_hbm, skip_ref),
                (w_hbm, w_ref),
                (x_hbm, x_ref),
            )
        )
    ]
    for load in loads:
        load.start()

    barrier = pltpu.get_barrier_semaphore()
    for r in (1, 2, 3):
        pl.semaphore_signal(barrier, inc=1, device_id=dev(xor_peer(r)), device_id_type=MESH)

    @pl.when(has_next)
    def _():
        pl.semaphore_signal(barrier, inc=1, device_id=dev(me + 4), device_id_type=MESH)

        @pl.when(place == 3)
        def _():
            pl.semaphore_signal(barrier, inc=1, device_id=dev(me + 1), device_id_type=MESH)

    @pl.when(has_prev)
    def _():
        pl.semaphore_signal(barrier, inc=1, device_id=dev(me - 4), device_id_type=MESH)

        @pl.when(place == 0)
        def _():
            pl.semaphore_signal(barrier, inc=1, device_id=dev(me - 1), device_id_type=MESH)

    next_count = 1 - (quad + 1) // quads
    prev_count = (quad + quads - 1) // quads
    pl.semaphore_wait(
        barrier,
        3 + next_count * (1 + place // 3) + prev_count * (2 - (place + 3) // 4),
    )

    def remote(src, dst, sems, j, target):
        return pltpu.make_async_remote_copy(
            src_ref=src, dst_ref=dst, send_sem=sems.at[0, j], recv_sem=sems.at[1, j],
            device_id=dev(target), device_id_type=MESH,
        )

    def halo_copy():
        return remote(x_hbm.at[pl.ds(rows - 8, 8)], halo, halo_sems, 0, me + 1)

    @pl.when(me < n_seq - 1)
    def _():
        halo_copy().start()

    for load in loads[:3]:
        load.wait()
    step = softplus(sl_ref[...])
    eye = lax.broadcasted_iota(jnp.int32, (heads, heads), 0) == lax.broadcasted_iota(
        jnp.int32, (heads, heads), 1
    )
    rate = jnp.sum(jnp.where(eye, -jnp.exp(dl_ref[...]), 0.0), axis=1, keepdims=True)
    row_id = lax.broadcasted_iota(jnp.int32, (rows, rows), 0)
    col_id = lax.broadcasted_iota(jnp.int32, (rows, rows), 1)
    upto = (row_id <= col_id).astype(F32)
    cum_t = jnp.dot(
        step * rate, upto, preferred_element_type=F32, precision=lax.Precision.HIGHEST
    )
    cum_end = cum_t[:, rows - 1 : rows]
    tot[0] = jnp.broadcast_to(cum_end, (heads, HEADDIM))
    for r in (1, 2, 3):
        remote(tot.at[0], tot.at[r], tot_sems, r, xor_peer(r)).start()
    gain = jnp.sum(jnp.where(eye, skip_ref[...], 0.0), axis=1, keepdims=True)
    gains[...] = jnp.broadcast_to(gain, (heads, HEADDIM))
    rowg[...] = cum_t - jnp.log(step)
    cum = jnp.transpose(cum_t)
    tail = jnp.transpose(jnp.exp(cum_end - cum_t) * step)
    for h in range(heads):
        tail_tab[h] = jnp.broadcast_to(tail[:, h : h + 1], (rows, HEADDIM))
        cum_tab[h] = jnp.broadcast_to(cum[:, h : h + 1], (rows, HEADDIM))

    for load in loads[3:]:
        load.wait()

    @pl.when(me == 0)
    def _():
        halo[...] = jnp.zeros_like(halo)

    @pl.when(me > 0)
    def _():
        halo_copy().wait_recv()

    def conv(start, slot):
        cols = pl.ds(start, PAIR)
        ext[slot, 0:8, :] = halo[:, cols].astype(F32)
        ext[slot, 8 : 8 + rows, :] = x_ref[:, cols].astype(F32)
        total = w_ref[0:1, cols] * ext[slot, pl.ds(9 - taps, rows), :]
        for k in range(1, taps):
            total = total + w_ref[k : k + 1, cols] * ext[slot, pl.ds(9 - taps + k, rows), :]
        half_v = 0.5 * total
        return (half_v + half_v * jnp.tanh(half_v)).astype(BF16)

    maps = conv(inner, 0)
    b_rows = maps[:, :STATE]
    c_rows = maps[:, STATE:]
    b_trans = jnp.transpose(b_rows.astype(F32)).astype(BF16)
    b_t[...] = b_trans
    c_act[...] = c_rows
    raw = jnp.dot(c_rows, b_trans, preferred_element_type=F32)
    scores[...] = jnp.where(row_id >= col_id, raw, 0.0)

    own_first = half * core
    other_first = half * (1 - core)

    def pair_state(i, slot):
        a = conv(pl.multiple_of(i * PAIR, PAIR), slot)
        act[i] = a
        left = a[:, :HEADDIM].astype(F32) * tail_tab[2 * i]
        right = a[:, HEADDIM:].astype(F32) * tail_tab[2 * i + 1]
        weighted = jnp.concatenate([left.astype(BF16), right.astype(BF16)], axis=1)
        return jnp.dot(b_t[...], weighted, preferred_element_type=F32)

    def s_copy(j):
        return remote(s_send.at[j], s_recv.at[j], s_sems, j, xor_peer(1))

    def t_copy(j):
        return remote(t_send.at[j], t_recv.at[j], t_sems, j, xor_peer(2))

    def p_copy(j):
        return remote(p_send.at[j], p_recv.at[j], p_sems, j, me + 4)

    def e_copy(j):
        return remote(e_send.at[j], e_recv.at[j], e_sems, j, xor_peer(1))

    def logs(r, j):
        h = 2 * (own_first + j)
        return jnp.concatenate([tot[r, pl.ds(h, 1), :], tot[r, pl.ds(h + 1, 1), :]], axis=1)

    def first_state(j):
        return jnp.where(core == 0, s_own[j], s_recv[j].astype(F32))

    def chip_step(j):
        s_copy(j).wait_recv()
        mine, got = s_own[j], s_recv[j].astype(F32)
        decay_last = jnp.exp(jnp.where(core == 0, logs(1, j), logs(0, j)))
        total = decay_last * jnp.where(core == 0, mine, got) + jnp.where(core == 0, got, mine)
        t_own[j] = total
        t_send[j] = total.astype(BF16)
        t_copy(j).start()

    for r in (1, 2, 3):
        remote(tot.at[0], tot.at[r], tot_sems, r, xor_peer(r)).wait_recv()

    @pl.loop(0, half)
    def _(j):
        s_send[j] = pair_state(other_first + j, 0).astype(BF16)
        s_copy(j).start()
        s_own[j] = pair_state(own_first + j, 1)

        @pl.when(j >= 1)
        def _():
            chip_step(j - 1)

    chip_step(half - 1)

    def quad_step(j):
        t_copy(j).wait_recv()
        mine, got = t_own[j], t_recv[j].astype(F32)
        log_mine = logs(0, j) + logs(1, j)
        log_got = logs(2, j) + logs(3, j)
        log_0 = jnp.where(side == 0, log_mine, log_got)
        log_1 = jnp.where(side == 0, log_got, log_mine)
        t_0 = jnp.where(side == 0, mine, got)
        t_1 = jnp.where(side == 0, got, mine)
        plane = jnp.exp(log_1) * t_0 + t_1

        @pl.when(has_prev)
        def _():
            p_copy(j).wait_recv()

        @pl.when(quad == 0)
        def _():
            p_recv[j] = jnp.zeros((STATE, PAIR), BF16)

        before = p_recv[j].astype(F32)

        @pl.when(has_next)
        def _():
            p_send[j] = (jnp.exp(log_0 + log_1) * before + plane).astype(BF16)
            p_copy(j).start()

        e_chip = jnp.where(side == 0, before, jnp.exp(log_0) * before + t_0)
        decay_first = jnp.exp(jnp.where(core == 0, logs(0, j), logs(1, j)))
        e_second = decay_first * e_chip + first_state(j)
        e_send[j] = jnp.where(core == 0, e_second, e_chip).astype(BF16)
        e_copy(j).start()
        ent[j] = jnp.where(core == 0, e_chip, e_second).astype(BF16)

    mid = rows // 2

    def intra(i):
        for u in range(2):
            h = 2 * i + u
            lanes = pl.ds(u * HEADDIM, HEADDIM)
            g = rowg[pl.ds(h, 1), :]
            col = cum_tab[h]
            v = act[i, :, lanes]
            gain = gains[pl.ds(h, 1), :]
            top = scores[0:mid, 0:mid] * jnp.exp(jnp.minimum(col[:mid] - g[:, :mid], 0.0))
            low_a = scores[mid:, 0:mid] * jnp.exp(jnp.minimum(col[mid:] - g[:, :mid], 0.0))
            low_b = scores[mid:, mid:] * jnp.exp(jnp.minimum(col[mid:] - g[:, mid:], 0.0))
            low = jnp.concatenate([low_a.astype(BF16), low_b.astype(BF16)], axis=1)
            y_top = jnp.dot(top.astype(BF16), v[:mid], preferred_element_type=F32)
            y_low = jnp.dot(low, v, preferred_element_type=F32)
            local[i, 0:mid, lanes] = y_top + gain * v[:mid].astype(F32)
            local[i, mid:, lanes] = y_low + gain * v[mid:].astype(F32)

    def finish(i, state):
        inter = jnp.dot(c_act[...], state, preferred_element_type=F32)
        grow = jnp.concatenate([jnp.exp(cum_tab[2 * i]), jnp.exp(cum_tab[2 * i + 1])], axis=1)
        out_ref[:, pl.ds(pl.multiple_of(i * PAIR, PAIR), PAIR)] = (
            local[i] + grow * inter
        ).astype(out_ref.dtype)

    def finish_step(j):
        finish(own_first + j, ent[j])
        e_copy(j).wait_recv()
        finish(other_first + j, e_recv[j])

    @pl.loop(0, half)
    def _(j):
        quad_step(j)
        intra(own_first + j)
        intra(other_first + j)

        @pl.when(j >= 1)
        def _():
            finish_step(j - 1)

    finish_step(half - 1)

    @pl.when(me < n_seq - 1)
    def _():
        halo_copy().wait_send()

    for r in (1, 2, 3):
        remote(tot.at[0], tot.at[r], tot_sems, r, xor_peer(r)).wait_send()

    @pl.loop(0, half)
    def _(j):
        s_copy(j).wait_send()
        t_copy(j).wait_send()
        e_copy(j).wait_send()

        @pl.when(has_next)
        def _():
            p_copy(j).wait_send()


def on_device(n_seq, conv_input, conv_weight, step_logit, decay_log, skip_gain):
    taps, channels = conv_weight.shape
    rows = conv_input.shape[0]
    heads = decay_log.shape[0]
    half = heads // 4
    vmem = pl.BlockSpec(memory_space=pltpu.VMEM)
    chunk = (half, STATE, PAIR)

    def pair_sems(count):
        return pltpu.SemaphoreType.DMA((2, count))

    return pl.pallas_call(
        functools.partial(kernel, n_seq, heads, rows, taps),
        out_shape=jax.ShapeDtypeStruct((rows, heads * HEADDIM), BF16),
        in_specs=[pl.BlockSpec(memory_space=pltpu.HBM)] * 5,
        out_specs=vmem,
        scratch_shapes=[
            pltpu.VMEM((rows, channels), BF16),
            pltpu.VMEM((taps, channels), F32),
            pltpu.VMEM((heads, rows), F32),
            pltpu.VMEM((1, heads), F32),
            pltpu.VMEM((1, heads), F32),
            pltpu.SemaphoreType.DMA((5,)),
            pltpu.VMEM((heads, HEADDIM), F32),
            pltpu.VMEM((8, channels), BF16),
            pltpu.VMEM((2, rows + 8, PAIR), F32),
            pltpu.VMEM((heads // 2, rows, PAIR), BF16),
            pltpu.VMEM((STATE, rows), BF16),
            pltpu.VMEM((rows, STATE), BF16),
            pltpu.VMEM((rows, rows), F32),
            pltpu.VMEM((heads, rows, HEADDIM), F32),
            pltpu.VMEM((heads, rows, HEADDIM), F32),
            pltpu.VMEM((heads, rows), F32),
            pltpu.VMEM((4, heads, HEADDIM), F32),
            pltpu.VMEM(chunk, BF16),
            pltpu.VMEM(chunk, F32),
            pltpu.VMEM(chunk, BF16),
            pltpu.VMEM(chunk, F32),
            pltpu.VMEM(chunk, BF16),
            pltpu.VMEM(chunk, BF16),
            pltpu.VMEM(chunk, BF16),
            pltpu.VMEM(chunk, BF16),
            pltpu.VMEM(chunk, BF16),
            pltpu.VMEM(chunk, BF16),
            pltpu.VMEM(chunk, BF16),
            pltpu.VMEM((heads // 2, rows, PAIR), F32),
            pair_sems(1),
            pair_sems(4),
            pair_sems(half),
            pair_sems(half),
            pair_sems(half),
            pair_sems(half),
        ],
        compiler_params=pltpu.CompilerParams(
            collective_id=0, has_side_effects=True, vmem_limit_bytes=48 * 1024 * 1024
        ),
    )(
        *(
            pltpu.with_memory_space_constraint(operand, pltpu.HBM)
            for operand in (
                conv_input,
                conv_weight,
                step_logit.T,
                decay_log.reshape(1, heads),
                skip_gain.reshape(1, heads),
            )
        )
    )


def solution(mesh):
    return jax.shard_map(
        functools.partial(on_device, mesh.shape["seq"]),
        mesh=mesh,
        in_specs=(P(("grp", "seq"), None), P(), P(("grp", "seq"), None), P(), P()),
        out_specs=P(("grp", "seq"), None),
        check_vma=False,
    )
```

```python
import functools

import jax
import jax.numpy as jnp
from jax import lax
from jax.experimental import pallas as pl
from jax.experimental.pallas import tpu as pltpu
from jax.sharding import PartitionSpec as P

HEADDIM = 128
STATE = 128
PAIR = 2 * HEADDIM
MESH = pl.DeviceIdType.MESH
F32 = jnp.float32
BF16 = jnp.bfloat16


def softplus(x):
    e = jnp.exp(-jnp.abs(x))
    series = e * (1.0 - e * (1 / 2 - e * (1 / 3 - e * (1 / 4 - e * (1 / 5 - e * (1 / 6))))))
    return jnp.maximum(x, 0.0) + jnp.where(e < 0.03, series, jnp.log(1.0 + e))


def kernel(
    n_seq, heads, rows, taps,
    x_hbm, w_hbm, sl_hbm, dl_hbm, skip_hbm, out_ref,
    x_ref, w_ref, sl_ref, dl_ref, skip_ref, load_sems,
    gains, halo, ext, act, b_t, c_act, scores, tail_tab, cum_tab, rowg, tot, cum_cols, plane,
    s_send, s_own, s_recv, t_own, t_send, t_recv, p_send, p_recv, g_send, g_recv, e_send, e_recv, ent, local,
    halo_sems, tot_sems, s_sems, t_sems, p_sems, g_sems, e_sems,
):
    me = lax.axis_index("seq")
    grp = lax.axis_index("grp")
    core = me % 2
    side = (me // 2) % 2
    quad = me // 4
    quads = n_seq // 4
    place = me % 4
    half = heads // 4
    inner = heads * HEADDIM
    has_next = quad < quads - 1
    has_prev = quad > 0

    def xor_peer(r):
        flip_core = (1 - 2 * core) * (r % 2)
        flip_side = (1 - 2 * side) * (r // 2) * 2
        return me + flip_core + flip_side

    def dev(seq_index):
        return (grp, seq_index)

    loads = [
        pltpu.make_async_copy(source, target, load_sems.at[k])
        for k, (source, target) in enumerate(
            (
                (sl_hbm, sl_ref),
                (dl_hbm, dl_ref),
                (skip_hbm, skip_ref),
                (w_hbm, w_ref),
                (x_hbm, x_ref),
            )
        )
    ]
    for load in loads:
        load.start()

    barrier = pltpu.get_barrier_semaphore()
    for r in (1, 2, 3):
        pl.semaphore_signal(barrier, inc=1, device_id=dev(xor_peer(r)), device_id_type=MESH)

    @pl.when(has_next)
    def _():
        pl.semaphore_signal(barrier, inc=1, device_id=dev(me + 4), device_id_type=MESH)

        @pl.when(place == 3)
        def _():
            pl.semaphore_signal(barrier, inc=1, device_id=dev(me + 1), device_id_type=MESH)

    @pl.when(has_prev)
    def _():
        pl.semaphore_signal(barrier, inc=1, device_id=dev(me - 4), device_id_type=MESH)

        @pl.when(place == 0)
        def _():
            pl.semaphore_signal(barrier, inc=1, device_id=dev(me - 1), device_id_type=MESH)

    def remote(src, dst, sems, j, target):
        return pltpu.make_async_remote_copy(
            src_ref=src, dst_ref=dst, send_sem=sems.at[0, j], recv_sem=sems.at[1, j],
            device_id=dev(target), device_id_type=MESH,
        )

    def halo_copy():
        return remote(x_hbm.at[pl.ds(rows - 8, 8)], halo, halo_sems, 0, me + 1)

    for load in loads[:3]:
        load.wait()
    step = softplus(sl_ref[...])
    eye = lax.broadcasted_iota(jnp.int32, (heads, heads), 0) == lax.broadcasted_iota(
        jnp.int32, (heads, heads), 1
    )
    rate = jnp.sum(jnp.where(eye, -jnp.exp(dl_ref[...]), 0.0), axis=1, keepdims=True)
    row_id = lax.broadcasted_iota(jnp.int32, (rows, rows), 0)
    col_id = lax.broadcasted_iota(jnp.int32, (rows, rows), 1)
    upto = (row_id <= col_id).astype(F32)
    cum_t = jnp.dot(
        step * rate, upto, preferred_element_type=F32, precision=lax.Precision.HIGHEST
    )
    cum_end = cum_t[:, rows - 1 : rows]
    tot[0] = jnp.broadcast_to(cum_end, (heads, HEADDIM))

    next_count = 1 - (quad + 1) // quads
    prev_count = (quad + quads - 1) // quads
    pl.semaphore_wait(
        barrier,
        3 + next_count * (1 + place // 3) + prev_count * (2 - (place + 3) // 4),
    )

    @pl.when(me < n_seq - 1)
    def _():
        halo_copy().start()

    for r in (1, 2, 3):
        remote(tot.at[0], tot.at[r], tot_sems, r, xor_peer(r)).start()
    gain = jnp.sum(jnp.where(eye, skip_ref[...], 0.0), axis=1, keepdims=True)
    gains[...] = jnp.broadcast_to(gain, (heads, HEADDIM))
    rowg[...] = cum_t - jnp.log(step)
    cum_cols[...] = jnp.transpose(cum_t)
    tail = jnp.transpose(jnp.exp(cum_end - cum_t) * step)
    for h in range(heads):
        tail_tab[h] = jnp.broadcast_to(tail[:, h : h + 1], (rows, HEADDIM))

    for load in loads[3:]:
        load.wait()

    @pl.when(me == 0)
    def _():
        halo[...] = jnp.zeros_like(halo)

    @pl.when(me > 0)
    def _():
        halo_copy().wait_recv()

    def conv(start, slot):
        cols = pl.ds(start, PAIR)
        ext[slot, 0:8, :] = halo[:, cols].astype(F32)
        ext[slot, 8 : 8 + rows, :] = x_ref[:, cols].astype(F32)
        total = w_ref[0:1, cols] * ext[slot, pl.ds(9 - taps, rows), :]
        for k in range(1, taps):
            total = total + w_ref[k : k + 1, cols] * ext[slot, pl.ds(9 - taps + k, rows), :]
        half_v = 0.5 * total
        return (half_v + half_v * jnp.tanh(half_v)).astype(BF16)

    maps = conv(inner, 0)
    b_rows = maps[:, :STATE]
    c_rows = maps[:, STATE:]
    b_trans = jnp.transpose(b_rows.astype(F32)).astype(BF16)
    b_t[...] = b_trans
    c_act[...] = c_rows

    own_first = half * core
    other_first = half * (1 - core)
    steps = half // 2

    def pair_of(first, j):
        flip = 1 - j % 2
        return first + steps * (side + flip * (1 - 2 * side)) + j // 2

    def pair_state(i, slot):
        a = conv(pl.multiple_of(i * PAIR, PAIR), slot)
        act[i] = a
        left = a[:, :HEADDIM].astype(F32) * tail_tab[2 * i]
        right = a[:, HEADDIM:].astype(F32) * tail_tab[2 * i + 1]
        weighted = jnp.concatenate([left.astype(BF16), right.astype(BF16)], axis=1)
        return jnp.dot(b_t[...], weighted, preferred_element_type=F32)

    def s_copy(j):
        return remote(s_send.at[j], s_recv.at[j], s_sems, j, xor_peer(1))

    def t_copy(m):
        return remote(t_send.at[m], t_recv.at[m], t_sems, m, xor_peer(2))

    def p_copy(m):
        return remote(p_send.at[m], p_recv.at[m], p_sems, m, me + 4)

    def g_copy(m):
        return remote(g_send.at[m], g_recv.at[m], g_sems, m, xor_peer(2))

    def e_copy(j):
        return remote(e_send.at[j], e_recv.at[j], e_sems, j, xor_peer(1))

    def logs(r, j):
        h = 2 * pair_of(own_first, j)
        return jnp.concatenate([tot[r, pl.ds(h, 1), :], tot[r, pl.ds(h + 1, 1), :]], axis=1)

    def local_states(j):
        s_send[j] = pair_state(pair_of(other_first, j), 0).astype(BF16)
        s_copy(j).start()
        s_own[j] = pair_state(pair_of(own_first, j), 1)

    def chip_total(j):
        s_copy(j).wait_recv()
        mine, got = s_own[j], s_recv[j].astype(F32)
        decay_last = jnp.exp(jnp.where(core == 0, logs(1, j), logs(0, j)))
        return decay_last * jnp.where(core == 0, mine, got) + jnp.where(core == 0, got, mine)

    def core_step(j, e_chip):
        decay_first = jnp.exp(jnp.where(core == 0, logs(0, j), logs(1, j)))
        first = jnp.where(core == 0, s_own[j], s_recv[j].astype(F32))
        e_second = decay_first * e_chip + first
        e_send[j] = jnp.where(core == 0, e_second, e_chip).astype(BF16)
        e_copy(j).start()
        ent[j] = jnp.where(core == 0, e_chip, e_second).astype(BF16)

    for r in (1, 2, 3):
        remote(tot.at[0], tot.at[r], tot_sems, r, xor_peer(r)).wait_recv()

    def quad_step(m):
        j = 2 * m + 1
        t_copy(m).wait_recv()
        mine, got = t_own[m], t_recv[m].astype(F32)
        log_mine = logs(0, j) + logs(1, j)
        log_got = logs(2, j) + logs(3, j)
        log_0 = jnp.where(side == 0, log_mine, log_got)
        log_1 = jnp.where(side == 0, log_got, log_mine)
        t_0 = jnp.where(side == 0, mine, got)
        t_1 = jnp.where(side == 0, got, mine)
        t_own[m] = t_0
        plane[...] = jnp.exp(log_1) * t_0 + t_1

        @pl.when(has_prev)
        def _():
            p_copy(m).wait_recv()

        @pl.when(quad == 0)
        def _():
            p_recv[m] = jnp.zeros((STATE, PAIR), BF16)

        before = p_recv[m].astype(F32)

        @pl.when(has_next)
        def _():
            p_send[m] = (jnp.exp(log_0 + log_1) * before + plane[...]).astype(BF16)
            p_copy(m).start()

        e_second = jnp.exp(log_0) * before + t_own[m]
        g_send[m] = jnp.where(side == 0, e_second, before).astype(BF16)
        g_copy(m).start()
        core_step(j, jnp.where(side == 0, before, e_second))

    mid = rows // 2

    def intra(i):
        for u in range(2):
            h = 2 * i + u
            lanes = pl.ds(u * HEADDIM, HEADDIM)
            g = rowg[pl.ds(h, 1), :]
            col = cum_tab[h]
            v = act[i, :, lanes]
            gain = gains[pl.ds(h, 1), :]
            top = scores[0:mid, 0:mid] * jnp.exp(jnp.minimum(col[:mid] - g[:, :mid], 0.0))
            low_a = scores[mid:, 0:mid] * jnp.exp(jnp.minimum(col[mid:] - g[:, :mid], 0.0))
            low_b = scores[mid:, mid:] * jnp.exp(jnp.minimum(col[mid:] - g[:, mid:], 0.0))
            low = jnp.concatenate([low_a.astype(BF16), low_b.astype(BF16)], axis=1)
            y_top = jnp.dot(top.astype(BF16), v[:mid], preferred_element_type=F32)
            y_low = jnp.dot(low, v, preferred_element_type=F32)
            local[i, 0:mid, lanes] = y_top + gain * v[:mid].astype(F32)
            local[i, mid:, lanes] = y_low + gain * v[mid:].astype(F32)

    def finish(i, state):
        inter = jnp.dot(c_act[...], state, preferred_element_type=F32)
        grow = jnp.concatenate([jnp.exp(cum_tab[2 * i]), jnp.exp(cum_tab[2 * i + 1])], axis=1)
        out_ref[:, pl.ds(pl.multiple_of(i * PAIR, PAIR), PAIR)] = (
            local[i] + grow * inter
        ).astype(out_ref.dtype)

    def finish_step(j):
        finish(pair_of(own_first, j), ent[j])
        e_copy(j).wait_recv()
        finish(pair_of(other_first, j), e_recv[j])

    most = 2 * steps
    lag = jnp.minimum(steps - 2 + 2 * quad, most)

    @pl.loop(0, most + steps + 2)
    def _(t):
        @pl.when((t >= 1) & (t < steps + 1))
        def _():
            t_send[t - 1] = chip_total(2 * t - 2).astype(BF16)
            t_copy(t - 1).start()

        @pl.when(t < steps)
        def _():
            local_states(2 * t)

        @pl.when((t >= 1) & (t < steps + 1))
        def _():
            t_own[t - 1] = chip_total(2 * t - 1)

        @pl.when((t >= lag) & (t < lag + steps))
        def _():
            quad_step(t - lag)

        @pl.when((t >= lag + 1) & (t < lag + 1 + steps))
        def _():
            m = t - lag - 1
            g_copy(m).wait_recv()
            core_step(2 * m, g_recv[m].astype(F32))

        @pl.when(t < steps)
        def _():
            local_states(2 * t + 1)

        @pl.when(t == steps)
        def _():
            raw = jnp.dot(c_act[...], b_t[...], preferred_element_type=F32)
            scores[...] = jnp.where(row_id >= col_id, raw, 0.0)
            cum = cum_cols[...]
            for h in range(heads):
                cum_tab[h] = jnp.broadcast_to(cum[:, h : h + 1], (rows, HEADDIM))

        @pl.when((t >= steps) & (t < 2 * steps))
        def _():
            @pl.loop(0, 2)
            def _(u):
                j = 2 * (t - steps) + u
                intra(pair_of(own_first, j))
                intra(pair_of(other_first, j))

        @pl.when((t >= lag + 2) & (t < lag + 2 + steps))
        def _():
            m = t - lag - 2
            finish_step(2 * m + 1)
            finish_step(2 * m)

    @pl.when(me < n_seq - 1)
    def _():
        halo_copy().wait_send()

    for r in (1, 2, 3):
        remote(tot.at[0], tot.at[r], tot_sems, r, xor_peer(r)).wait_send()

    @pl.loop(0, half)
    def _(j):
        s_copy(j).wait_send()
        e_copy(j).wait_send()

    @pl.loop(0, steps)
    def _(m):
        t_copy(m).wait_send()
        g_copy(m).wait_send()

        @pl.when(has_next)
        def _():
            p_copy(m).wait_send()


def on_device(n_seq, conv_input, conv_weight, step_logit, decay_log, skip_gain):
    taps, channels = conv_weight.shape
    rows = conv_input.shape[0]
    heads = decay_log.shape[0]
    half = heads // 4
    vmem = pl.BlockSpec(memory_space=pltpu.VMEM)
    chunk = (half, STATE, PAIR)
    part = (half // 2, STATE, PAIR)

    def pair_sems(count):
        return pltpu.SemaphoreType.DMA((2, count))

    return pl.pallas_call(
        functools.partial(kernel, n_seq, heads, rows, taps),
        out_shape=jax.ShapeDtypeStruct((rows, heads * HEADDIM), BF16),
        in_specs=[pl.BlockSpec(memory_space=pltpu.HBM)] * 5,
        out_specs=vmem,
        scratch_shapes=[
            pltpu.VMEM((rows, channels), BF16),
            pltpu.VMEM((taps, channels), F32),
            pltpu.VMEM((heads, rows), F32),
            pltpu.VMEM((1, heads), F32),
            pltpu.VMEM((1, heads), F32),
            pltpu.SemaphoreType.DMA((5,)),
            pltpu.VMEM((heads, HEADDIM), F32),
            pltpu.VMEM((8, channels), BF16),
            pltpu.VMEM((2, rows + 8, PAIR), F32),
            pltpu.VMEM((heads // 2, rows, PAIR), BF16),
            pltpu.VMEM((STATE, rows), BF16),
            pltpu.VMEM((rows, STATE), BF16),
            pltpu.VMEM((rows, rows), F32),
            pltpu.VMEM((heads, rows, HEADDIM), F32),
            pltpu.VMEM((heads, rows, HEADDIM), F32),
            pltpu.VMEM((heads, rows), F32),
            pltpu.VMEM((4, heads, HEADDIM), F32),
            pltpu.VMEM((rows, heads), F32),
            pltpu.VMEM((STATE, PAIR), F32),
            pltpu.VMEM(chunk, BF16),
            pltpu.VMEM(chunk, F32),
            pltpu.VMEM(chunk, BF16),
            pltpu.VMEM(part, F32),
            pltpu.VMEM(part, BF16),
            pltpu.VMEM(part, BF16),
            pltpu.VMEM(part, BF16),
            pltpu.VMEM(part, BF16),
            pltpu.VMEM(part, BF16),
            pltpu.VMEM(part, BF16),
            pltpu.VMEM(chunk, BF16),
            pltpu.VMEM(chunk, BF16),
            pltpu.VMEM(chunk, BF16),
            pltpu.VMEM((heads // 2, rows, PAIR), F32),
            pair_sems(1),
            pair_sems(4),
            pair_sems(half),
            pair_sems(half // 2),
            pair_sems(half // 2),
            pair_sems(half // 2),
            pair_sems(half),
        ],
        compiler_params=pltpu.CompilerParams(
            collective_id=0, has_side_effects=True, vmem_limit_bytes=48 * 1024 * 1024
        ),
    )(
        *(
            pltpu.with_memory_space_constraint(operand, pltpu.HBM)
            for operand in (
                conv_input,
                conv_weight,
                step_logit.T,
                decay_log.reshape(1, heads),
                skip_gain.reshape(1, heads),
            )
        )
    )


def solution(mesh):
    return jax.shard_map(
        functools.partial(on_device, mesh.shape["seq"]),
        mesh=mesh,
        in_specs=(P(("grp", "seq"), None), P(), P(("grp", "seq"), None), P(), P()),
        out_specs=P(("grp", "seq"), None),
        check_vma=False,
    )
```

```python
import functools

import jax
import jax.numpy as jnp
from jax import lax
from jax.experimental import pallas as pl
from jax.experimental.pallas import tpu as pltpu
from jax.sharding import PartitionSpec as P

HEADDIM = 128
STATE = 128
PAIR = 2 * HEADDIM
MESH = pl.DeviceIdType.MESH
F32 = jnp.float32
BF16 = jnp.bfloat16


def softplus(x):
    e = jnp.exp(-jnp.abs(x))
    series = e * (1.0 - e * (1 / 2 - e * (1 / 3 - e * (1 / 4 - e * (1 / 5 - e * (1 / 6))))))
    return jnp.maximum(x, 0.0) + jnp.where(e < 0.03, series, jnp.log(1.0 + e))


def kernel(
    n_seq, heads, rows, taps,
    x_hbm, w_hbm, sl_hbm, dl_hbm, skip_hbm, out_ref,
    x_ref, w_ref, sl_ref, dl_ref, skip_ref, load_sems,
    gains, halo, ext, act, b_t, c_act, scores, tail_tab, cum_tab, rowg, tot, cum_cols, plane,
    s_send, s_own, s_recv, t_own, t_send, t_recv, p_send, p_recv, g_send, g_recv, e_send, e_recv, ent, local,
    halo_sems, tot_sems, s_sems, t_sems, p_sems, g_sems, e_sems,
):
    me = lax.axis_index("seq")
    grp = lax.axis_index("grp")
    core = me % 2
    side = (me // 2) % 2
    quad = me // 4
    quads = n_seq // 4
    place = me % 4
    half = heads // 4
    inner = heads * HEADDIM
    has_next = quad < quads - 1
    has_prev = quad > 0

    def xor_peer(r):
        flip_core = (1 - 2 * core) * (r % 2)
        flip_side = (1 - 2 * side) * (r // 2) * 2
        return me + flip_core + flip_side

    def dev(seq_index):
        return (grp, seq_index)

    loads = [
        pltpu.make_async_copy(source, target, load_sems.at[k])
        for k, (source, target) in enumerate(
            (
                (sl_hbm, sl_ref),
                (dl_hbm, dl_ref),
                (skip_hbm, skip_ref),
                (w_hbm, w_ref),
                (x_hbm, x_ref),
            )
        )
    ]
    for load in loads:
        load.start()

    barrier = pltpu.get_barrier_semaphore()
    for r in (1, 2, 3):
        pl.semaphore_signal(barrier, inc=1, device_id=dev(xor_peer(r)), device_id_type=MESH)

    @pl.when(has_next)
    def _():
        pl.semaphore_signal(barrier, inc=1, device_id=dev(me + 4), device_id_type=MESH)

        @pl.when(place == 3)
        def _():
            pl.semaphore_signal(barrier, inc=1, device_id=dev(me + 1), device_id_type=MESH)

    @pl.when(has_prev)
    def _():
        pl.semaphore_signal(barrier, inc=1, device_id=dev(me - 4), device_id_type=MESH)

        @pl.when(place == 0)
        def _():
            pl.semaphore_signal(barrier, inc=1, device_id=dev(me - 1), device_id_type=MESH)

    def remote(src, dst, sems, j, target):
        return pltpu.make_async_remote_copy(
            src_ref=src, dst_ref=dst, send_sem=sems.at[0, j], recv_sem=sems.at[1, j],
            device_id=dev(target), device_id_type=MESH,
        )

    def halo_copy():
        return remote(x_hbm.at[pl.ds(rows - 8, 8)], halo, halo_sems, 0, me + 1)

    for load in loads[:3]:
        load.wait()
    next_count = 1 - (quad + 1) // quads
    prev_count = (quad + quads - 1) // quads
    pl.semaphore_wait(
        barrier,
        3 + next_count * (1 + place // 3) + prev_count * (2 - (place + 3) // 4),
    )

    @pl.when(me < n_seq - 1)
    def _():
        halo_copy().start()

    step = softplus(sl_ref[...])
    eye = lax.broadcasted_iota(jnp.int32, (heads, heads), 0) == lax.broadcasted_iota(
        jnp.int32, (heads, heads), 1
    )
    rate = jnp.sum(jnp.where(eye, -jnp.exp(dl_ref[...]), 0.0), axis=1, keepdims=True)
    row_id = lax.broadcasted_iota(jnp.int32, (rows, rows), 0)
    col_id = lax.broadcasted_iota(jnp.int32, (rows, rows), 1)
    upto = (row_id <= col_id).astype(F32)
    cum_t = jnp.dot(
        step * rate, upto, preferred_element_type=F32, precision=lax.Precision.HIGHEST
    )
    cum_end = cum_t[:, rows - 1 : rows]
    tot[0] = jnp.broadcast_to(cum_end, (heads, HEADDIM))

    for r in (1, 2, 3):
        remote(tot.at[0], tot.at[r], tot_sems, r, xor_peer(r)).start()
    gain = jnp.sum(jnp.where(eye, skip_ref[...], 0.0), axis=1, keepdims=True)
    gains[...] = jnp.broadcast_to(gain, (heads, HEADDIM))
    rowg[...] = cum_t - jnp.log(step)
    cum_cols[...] = jnp.transpose(cum_t)
    tail = jnp.transpose(jnp.exp(cum_end - cum_t) * step)
    for h in range(heads):
        tail_tab[h] = jnp.broadcast_to(tail[:, h : h + 1], (rows, HEADDIM))

    for load in loads[3:]:
        load.wait()

    @pl.when(me == 0)
    def _():
        halo[...] = jnp.zeros_like(halo)

    @pl.when(me > 0)
    def _():
        halo_copy().wait_recv()

    def conv(start, slot):
        cols = pl.ds(start, PAIR)
        ext[slot, 0:8, :] = halo[:, cols].astype(F32)
        ext[slot, 8 : 8 + rows, :] = x_ref[:, cols].astype(F32)
        total = w_ref[0:1, cols] * ext[slot, pl.ds(9 - taps, rows), :]
        for k in range(1, taps):
            total = total + w_ref[k : k + 1, cols] * ext[slot, pl.ds(9 - taps + k, rows), :]
        half_v = 0.5 * total
        return (half_v + half_v * jnp.tanh(half_v)).astype(BF16)

    maps = conv(inner, 0)
    b_rows = maps[:, :STATE]
    c_rows = maps[:, STATE:]
    b_trans = jnp.transpose(b_rows.astype(F32)).astype(BF16)
    b_t[...] = b_trans
    c_act[...] = c_rows

    own_first = half * core
    other_first = half * (1 - core)
    steps = half // 2

    def pair_of(first, j):
        flip = 1 - j % 2
        return first + steps * (side + flip * (1 - 2 * side)) + j // 2

    def pair_state(i, slot):
        a = conv(pl.multiple_of(i * PAIR, PAIR), slot)
        act[i] = a
        left = a[:, :HEADDIM].astype(F32) * tail_tab[2 * i]
        right = a[:, HEADDIM:].astype(F32) * tail_tab[2 * i + 1]
        weighted = jnp.concatenate([left.astype(BF16), right.astype(BF16)], axis=1)
        return jnp.dot(b_t[...], weighted, preferred_element_type=F32)

    def s_copy(j):
        return remote(s_send.at[j], s_recv.at[j], s_sems, j, xor_peer(1))

    def t_copy(m):
        return remote(t_send.at[m], t_recv.at[m], t_sems, m, xor_peer(2))

    def p_copy(m):
        return remote(p_send.at[m], p_recv.at[m], p_sems, m, me + 4)

    def g_copy(m):
        return remote(g_send.at[m], g_recv.at[m], g_sems, m, xor_peer(2))

    def e_copy(j):
        return remote(e_send.at[j], e_recv.at[j], e_sems, j, xor_peer(1))

    def logs(r, j):
        h = 2 * pair_of(own_first, j)
        return jnp.concatenate([tot[r, pl.ds(h, 1), :], tot[r, pl.ds(h + 1, 1), :]], axis=1)

    def local_states(j):
        s_send[j] = pair_state(pair_of(other_first, j), 0).astype(BF16)
        s_copy(j).start()
        s_own[j] = pair_state(pair_of(own_first, j), 1)

    def chip_total(j):
        s_copy(j).wait_recv()
        mine, got = s_own[j], s_recv[j].astype(F32)
        decay_last = jnp.exp(jnp.where(core == 0, logs(1, j), logs(0, j)))
        return decay_last * jnp.where(core == 0, mine, got) + jnp.where(core == 0, got, mine)

    def core_step(j, e_chip):
        decay_first = jnp.exp(jnp.where(core == 0, logs(0, j), logs(1, j)))
        first = jnp.where(core == 0, s_own[j], s_recv[j].astype(F32))
        e_second = decay_first * e_chip + first
        e_send[j] = jnp.where(core == 0, e_second, e_chip).astype(BF16)
        e_copy(j).start()
        ent[j] = jnp.where(core == 0, e_chip, e_second).astype(BF16)

    for r in (1, 2, 3):
        remote(tot.at[0], tot.at[r], tot_sems, r, xor_peer(r)).wait_recv()

    def quad_step(m):
        j = 2 * m + 1
        t_copy(m).wait_recv()
        mine, got = t_own[m], t_recv[m].astype(F32)
        log_mine = logs(0, j) + logs(1, j)
        log_got = logs(2, j) + logs(3, j)
        log_0 = jnp.where(side == 0, log_mine, log_got)
        log_1 = jnp.where(side == 0, log_got, log_mine)
        t_0 = jnp.where(side == 0, mine, got)
        t_1 = jnp.where(side == 0, got, mine)
        t_own[m] = t_0
        plane[...] = jnp.exp(log_1) * t_0 + t_1

        @pl.when(has_prev)
        def _():
            p_copy(m).wait_recv()

        @pl.when(quad == 0)
        def _():
            p_recv[m] = jnp.zeros((STATE, PAIR), BF16)

        before = p_recv[m].astype(F32)

        @pl.when(has_next)
        def _():
            p_send[m] = (jnp.exp(log_0 + log_1) * before + plane[...]).astype(BF16)
            p_copy(m).start()

        e_second = jnp.exp(log_0) * before + t_own[m]
        g_send[m] = jnp.where(side == 0, e_second, before).astype(BF16)
        g_copy(m).start()
        core_step(j, jnp.where(side == 0, before, e_second))

    mid = rows // 2

    def intra(i):
        for u in range(2):
            h = 2 * i + u
            lanes = pl.ds(u * HEADDIM, HEADDIM)
            g = rowg[pl.ds(h, 1), :]
            col = cum_tab[h]
            v = act[i, :, lanes]
            gain = gains[pl.ds(h, 1), :]
            top = scores[0:mid, 0:mid] * jnp.exp(jnp.minimum(col[:mid] - g[:, :mid], 0.0))
            low_a = scores[mid:, 0:mid] * jnp.exp(jnp.minimum(col[mid:] - g[:, :mid], 0.0))
            low_b = scores[mid:, mid:] * jnp.exp(jnp.minimum(col[mid:] - g[:, mid:], 0.0))
            low = jnp.concatenate([low_a.astype(BF16), low_b.astype(BF16)], axis=1)
            y_top = jnp.dot(top.astype(BF16), v[:mid], preferred_element_type=F32)
            y_low = jnp.dot(low, v, preferred_element_type=F32)
            local[i, 0:mid, lanes] = y_top + gain * v[:mid].astype(F32)
            local[i, mid:, lanes] = y_low + gain * v[mid:].astype(F32)

    def finish(i, state):
        inter = jnp.dot(c_act[...], state, preferred_element_type=F32)
        grow = jnp.concatenate([jnp.exp(cum_tab[2 * i]), jnp.exp(cum_tab[2 * i + 1])], axis=1)
        out_ref[:, pl.ds(pl.multiple_of(i * PAIR, PAIR), PAIR)] = (
            local[i] + grow * inter
        ).astype(out_ref.dtype)

    def finish_step(j):
        finish(pair_of(own_first, j), ent[j])
        e_copy(j).wait_recv()
        finish(pair_of(other_first, j), e_recv[j])

    most = 2 * steps
    lag = jnp.minimum(steps - 2 + (3 * quad + 1) // 2, most)
    begin = steps + 2 * (1 - prev_count)
    end_lag = jnp.maximum(lag + 2, begin)

    @pl.loop(0, most + steps + 2)
    def _(t):
        @pl.when((t >= 1) & (t < steps + 1))
        def _():
            t_send[t - 1] = chip_total(2 * t - 2).astype(BF16)
            t_copy(t - 1).start()

        @pl.when(t < steps)
        def _():
            local_states(2 * t)

        @pl.when((t >= 1) & (t < steps + 1))
        def _():
            t_own[t - 1] = chip_total(2 * t - 1)

        @pl.when((t >= lag) & (t < lag + steps))
        def _():
            quad_step(t - lag)

        @pl.when((t >= lag + 1) & (t < lag + 1 + steps))
        def _():
            m = t - lag - 1
            g_copy(m).wait_recv()
            core_step(2 * m, g_recv[m].astype(F32))

        @pl.when(t < steps)
        def _():
            local_states(2 * t + 1)

        @pl.when(t == begin)
        def _():
            raw = jnp.dot(c_act[...], b_t[...], preferred_element_type=F32)
            scores[...] = jnp.where(row_id >= col_id, raw, 0.0)
            cum = cum_cols[...]
            for h in range(heads):
                cum_tab[h] = jnp.broadcast_to(cum[:, h : h + 1], (rows, HEADDIM))

        @pl.when((t >= begin) & (t < begin + steps))
        def _():
            @pl.loop(0, 2)
            def _(u):
                j = 2 * (t - begin) + u
                intra(pair_of(own_first, j))
                intra(pair_of(other_first, j))

        @pl.when((t >= end_lag) & (t < end_lag + steps))
        def _():
            m = t - end_lag
            finish_step(2 * m + 1)
            finish_step(2 * m)

    @pl.when(me < n_seq - 1)
    def _():
        halo_copy().wait_send()

    for r in (1, 2, 3):
        remote(tot.at[0], tot.at[r], tot_sems, r, xor_peer(r)).wait_send()

    @pl.loop(0, half)
    def _(j):
        s_copy(j).wait_send()
        e_copy(j).wait_send()

    @pl.loop(0, steps)
    def _(m):
        t_copy(m).wait_send()
        g_copy(m).wait_send()

        @pl.when(has_next)
        def _():
            p_copy(m).wait_send()


def on_device(n_seq, conv_input, conv_weight, step_logit, decay_log, skip_gain):
    taps, channels = conv_weight.shape
    rows = conv_input.shape[0]
    heads = decay_log.shape[0]
    half = heads // 4
    vmem = pl.BlockSpec(memory_space=pltpu.VMEM)
    chunk = (half, STATE, PAIR)
    part = (half // 2, STATE, PAIR)

    def pair_sems(count):
        return pltpu.SemaphoreType.DMA((2, count))

    return pl.pallas_call(
        functools.partial(kernel, n_seq, heads, rows, taps),
        out_shape=jax.ShapeDtypeStruct((rows, heads * HEADDIM), BF16),
        in_specs=[pl.BlockSpec(memory_space=pltpu.HBM)] * 5,
        out_specs=vmem,
        scratch_shapes=[
            pltpu.VMEM((rows, channels), BF16),
            pltpu.VMEM((taps, channels), F32),
            pltpu.VMEM((heads, rows), F32),
            pltpu.VMEM((1, heads), F32),
            pltpu.VMEM((1, heads), F32),
            pltpu.SemaphoreType.DMA((5,)),
            pltpu.VMEM((heads, HEADDIM), F32),
            pltpu.VMEM((8, channels), BF16),
            pltpu.VMEM((2, rows + 8, PAIR), F32),
            pltpu.VMEM((heads // 2, rows, PAIR), BF16),
            pltpu.VMEM((STATE, rows), BF16),
            pltpu.VMEM((rows, STATE), BF16),
            pltpu.VMEM((rows, rows), F32),
            pltpu.VMEM((heads, rows, HEADDIM), F32),
            pltpu.VMEM((heads, rows, HEADDIM), F32),
            pltpu.VMEM((heads, rows), F32),
            pltpu.VMEM((4, heads, HEADDIM), F32),
            pltpu.VMEM((rows, heads), F32),
            pltpu.VMEM((STATE, PAIR), F32),
            pltpu.VMEM(chunk, BF16),
            pltpu.VMEM(chunk, F32),
            pltpu.VMEM(chunk, BF16),
            pltpu.VMEM(part, F32),
            pltpu.VMEM(part, BF16),
            pltpu.VMEM(part, BF16),
            pltpu.VMEM(part, BF16),
            pltpu.VMEM(part, BF16),
            pltpu.VMEM(part, BF16),
            pltpu.VMEM(part, BF16),
            pltpu.VMEM(chunk, BF16),
            pltpu.VMEM(chunk, BF16),
            pltpu.VMEM(chunk, BF16),
            pltpu.VMEM((heads // 2, rows, PAIR), F32),
            pair_sems(1),
            pair_sems(4),
            pair_sems(half),
            pair_sems(half // 2),
            pair_sems(half // 2),
            pair_sems(half // 2),
            pair_sems(half),
        ],
        compiler_params=pltpu.CompilerParams(
            collective_id=0, has_side_effects=True, vmem_limit_bytes=48 * 1024 * 1024
        ),
    )(
        *(
            pltpu.with_memory_space_constraint(operand, pltpu.HBM)
            for operand in (
                conv_input,
                conv_weight,
                step_logit.T,
                decay_log.reshape(1, heads),
                skip_gain.reshape(1, heads),
            )
        )
    )


def solution(mesh):
    return jax.shard_map(
        functools.partial(on_device, mesh.shape["seq"]),
        mesh=mesh,
        in_specs=(P(("grp", "seq"), None), P(), P(("grp", "seq"), None), P(), P()),
        out_specs=P(("grp", "seq"), None),
        check_vma=False,
    )
```

```python
import functools

import jax
import jax.numpy as jnp
from jax import lax
from jax.experimental import pallas as pl
from jax.experimental.pallas import tpu as pltpu
from jax.sharding import PartitionSpec as P

HEADDIM = 128
STATE = 128
PAIR = 2 * HEADDIM
MESH = pl.DeviceIdType.MESH
F32 = jnp.float32
BF16 = jnp.bfloat16


def softplus(x):
    e = jnp.exp(-jnp.abs(x))
    series = e * (1.0 - e * (1 / 2 - e * (1 / 3 - e * (1 / 4 - e * (1 / 5 - e * (1 / 6))))))
    return jnp.maximum(x, 0.0) + jnp.where(e < 0.03, series, jnp.log(1.0 + e))


def kernel(
    n_seq, heads, rows, taps,
    x_hbm, w_hbm, sl_hbm, dl_hbm, skip_hbm, out_ref,
    x_ref, w_ref, sl_ref, dl_ref, skip_ref, load_sems,
    gains, halo, ext, act, b_t, c_act, scores, tail_tab, cum_tab, rowg, tot, cum_cols, plane,
    s_send, s_own, s_recv, t_own, t_send, t_recv, p_send, p_recv, g_send, g_recv, e_send, e_recv, ent, local,
    halo_sems, tot_sems, s_sems, t_sems, p_sems, g_sems, e_sems,
):
    me = lax.axis_index("seq")
    grp = lax.axis_index("grp")
    core = me % 2
    side = (me // 2) % 2
    quad = me // 4
    quads = n_seq // 4
    place = me % 4
    half = heads // 4
    inner = heads * HEADDIM
    has_next = quad < quads - 1
    has_prev = quad > 0

    def xor_peer(r):
        flip_core = (1 - 2 * core) * (r % 2)
        flip_side = (1 - 2 * side) * (r // 2) * 2
        return me + flip_core + flip_side

    def dev(seq_index):
        return (grp, seq_index)

    loads = [
        pltpu.make_async_copy(source, target, load_sems.at[k])
        for k, (source, target) in enumerate(
            (
                (sl_hbm, sl_ref),
                (dl_hbm, dl_ref),
                (skip_hbm, skip_ref),
                (w_hbm, w_ref),
                (x_hbm.at[:, inner:], x_ref.at[:, inner:]),
                (x_hbm.at[:, :inner], x_ref.at[:, :inner]),
            )
        )
    ]
    for load in loads:
        load.start()

    barrier = pltpu.get_barrier_semaphore()
    for r in (1, 2, 3):
        pl.semaphore_signal(barrier, inc=1, device_id=dev(xor_peer(r)), device_id_type=MESH)

    @pl.when(has_next)
    def _():
        pl.semaphore_signal(barrier, inc=1, device_id=dev(me + 4), device_id_type=MESH)

        @pl.when(place == 3)
        def _():
            pl.semaphore_signal(barrier, inc=1, device_id=dev(me + 1), device_id_type=MESH)

    @pl.when(has_prev)
    def _():
        pl.semaphore_signal(barrier, inc=1, device_id=dev(me - 4), device_id_type=MESH)

        @pl.when(place == 0)
        def _():
            pl.semaphore_signal(barrier, inc=1, device_id=dev(me - 1), device_id_type=MESH)

    def remote(src, dst, sems, j, target):
        return pltpu.make_async_remote_copy(
            src_ref=src, dst_ref=dst, send_sem=sems.at[0, j], recv_sem=sems.at[1, j],
            device_id=dev(target), device_id_type=MESH,
        )

    def halo_copy():
        return remote(x_hbm.at[pl.ds(rows - 8, 8)], halo, halo_sems, 0, me + 1)

    for load in loads[:3]:
        load.wait()
    step = softplus(sl_ref[...])
    eye = lax.broadcasted_iota(jnp.int32, (heads, heads), 0) == lax.broadcasted_iota(
        jnp.int32, (heads, heads), 1
    )
    rate = jnp.sum(jnp.where(eye, -jnp.exp(dl_ref[...]), 0.0), axis=1, keepdims=True)
    row_id = lax.broadcasted_iota(jnp.int32, (rows, rows), 0)
    col_id = lax.broadcasted_iota(jnp.int32, (rows, rows), 1)
    upto = (row_id <= col_id).astype(F32)
    cum_t = jnp.dot(
        step * rate, upto, preferred_element_type=F32, precision=lax.Precision.HIGHEST
    )
    cum_end = cum_t[:, rows - 1 : rows]
    tot[0] = jnp.broadcast_to(cum_end, (heads, HEADDIM))

    next_count = 1 - (quad + 1) // quads
    prev_count = (quad + quads - 1) // quads
    pl.semaphore_wait(
        barrier,
        3 + next_count * (1 + place // 3) + prev_count * (2 - (place + 3) // 4),
    )

    @pl.when(me < n_seq - 1)
    def _():
        halo_copy().start()

    for r in (1, 2, 3):
        remote(tot.at[0], tot.at[r], tot_sems, r, xor_peer(r)).start()
    gain = jnp.sum(jnp.where(eye, skip_ref[...], 0.0), axis=1, keepdims=True)
    gains[...] = jnp.broadcast_to(gain, (heads, HEADDIM))
    rowg[...] = cum_t - jnp.log(step)
    cum_cols[...] = jnp.transpose(cum_t)
    tail = jnp.transpose(jnp.exp(cum_end - cum_t) * step)
    for h in range(heads):
        tail_tab[h] = jnp.broadcast_to(tail[:, h : h + 1], (rows, HEADDIM))

    for load in loads[3:5]:
        load.wait()

    @pl.when(me == 0)
    def _():
        halo[...] = jnp.zeros_like(halo)

    @pl.when(me > 0)
    def _():
        halo_copy().wait_recv()

    def conv(start, slot):
        cols = pl.ds(start, PAIR)
        ext[slot, 0:8, :] = halo[:, cols].astype(F32)
        ext[slot, 8 : 8 + rows, :] = x_ref[:, cols].astype(F32)
        total = (0.5 * w_ref[0:1, cols]) * ext[slot, pl.ds(9 - taps, rows), :]
        for k in range(1, taps):
            total = total + (0.5 * w_ref[k : k + 1, cols]) * ext[slot, pl.ds(9 - taps + k, rows), :]
        half_v = total
        return (half_v + half_v * jnp.tanh(half_v)).astype(BF16)

    maps = conv(inner, 0)
    loads[5].wait()
    b_rows = maps[:, :STATE]
    c_rows = maps[:, STATE:]
    b_trans = jnp.transpose(b_rows.astype(F32)).astype(BF16)
    b_t[...] = b_trans
    c_act[...] = c_rows

    own_first = half * core
    other_first = half * (1 - core)
    steps = half // 2

    def pair_of(first, j):
        flip = 1 - j % 2
        return first + steps * (side + flip * (1 - 2 * side)) + j // 2

    def pair_state(i, slot):
        a = conv(pl.multiple_of(i * PAIR, PAIR), slot)
        act[i] = a
        left = a[:, :HEADDIM].astype(F32) * tail_tab[2 * i]
        right = a[:, HEADDIM:].astype(F32) * tail_tab[2 * i + 1]
        weighted = jnp.concatenate([left.astype(BF16), right.astype(BF16)], axis=1)
        return jnp.dot(b_t[...], weighted, preferred_element_type=F32)

    def s_copy(j):
        return remote(s_send.at[j], s_recv.at[j], s_sems, j, xor_peer(1))

    def t_copy(m):
        return remote(t_send.at[m], t_recv.at[m], t_sems, m, xor_peer(2))

    def p_copy(m):
        return remote(p_send.at[m], p_recv.at[m], p_sems, m, me + 4)

    def g_copy(m):
        return remote(g_send.at[m], g_recv.at[m], g_sems, m, xor_peer(2))

    def e_copy(j):
        return remote(e_send.at[j], e_recv.at[j], e_sems, j, xor_peer(1))

    def logs(r, j):
        h = 2 * pair_of(own_first, j)
        return jnp.concatenate([tot[r, pl.ds(h, 1), :], tot[r, pl.ds(h + 1, 1), :]], axis=1)

    def local_states(j):
        s_send[j] = pair_state(pair_of(other_first, j), 0).astype(BF16)
        s_copy(j).start()
        s_own[j] = pair_state(pair_of(own_first, j), 1)

    def chip_total(j):
        s_copy(j).wait_recv()
        mine, got = s_own[j], s_recv[j].astype(F32)
        decay_last = jnp.exp(jnp.where(core == 0, logs(1, j), logs(0, j)))
        return decay_last * jnp.where(core == 0, mine, got) + jnp.where(core == 0, got, mine)

    def core_step(j, e_chip):
        decay_first = jnp.exp(jnp.where(core == 0, logs(0, j), logs(1, j)))
        first = jnp.where(core == 0, s_own[j], s_recv[j].astype(F32))
        e_second = decay_first * e_chip + first
        e_send[j] = jnp.where(core == 0, e_second, e_chip).astype(BF16)
        e_copy(j).start()
        ent[j] = jnp.where(core == 0, e_chip, e_second).astype(BF16)

    def quad_step(m):
        j = 2 * m + 1
        t_copy(m).wait_recv()
        mine, got = t_own[m], t_recv[m].astype(F32)
        log_mine = logs(0, j) + logs(1, j)
        log_got = logs(2, j) + logs(3, j)
        log_0 = jnp.where(side == 0, log_mine, log_got)
        log_1 = jnp.where(side == 0, log_got, log_mine)
        t_0 = jnp.where(side == 0, mine, got)
        t_1 = jnp.where(side == 0, got, mine)
        t_own[m] = t_0
        plane[...] = jnp.exp(log_1) * t_0 + t_1

        @pl.when(has_prev)
        def _():
            p_copy(m).wait_recv()

        @pl.when(quad == 0)
        def _():
            p_recv[m] = jnp.zeros((STATE, PAIR), BF16)

        before = p_recv[m].astype(F32)

        @pl.when(has_next)
        def _():
            p_send[m] = (jnp.exp(log_0 + log_1) * before + plane[...]).astype(BF16)
            p_copy(m).start()

        e_second = jnp.exp(log_0) * before + t_own[m]
        g_send[m] = jnp.where(side == 0, e_second, before).astype(BF16)
        g_copy(m).start()
        core_step(j, jnp.where(side == 0, before, e_second))

    mid = rows // 2

    def intra(i):
        for u in range(2):
            h = 2 * i + u
            lanes = pl.ds(u * HEADDIM, HEADDIM)
            g = rowg[pl.ds(h, 1), :]
            col = cum_tab[h]
            v = act[i, :, lanes]
            gain = gains[pl.ds(h, 1), :]
            top = scores[0:mid, 0:mid] * jnp.exp(jnp.minimum(col[:mid] - g[:, :mid], 0.0))
            low_a = scores[mid:, 0:mid] * jnp.exp(jnp.minimum(col[mid:] - g[:, :mid], 0.0))
            low_b = scores[mid:, mid:] * jnp.exp(jnp.minimum(col[mid:] - g[:, mid:], 0.0))
            low = jnp.concatenate([low_a.astype(BF16), low_b.astype(BF16)], axis=1)
            y_top = jnp.dot(top.astype(BF16), v[:mid], preferred_element_type=F32)
            y_low = jnp.dot(low, v, preferred_element_type=F32)
            local[i, 0:mid, lanes] = y_top + gain * v[:mid].astype(F32)
            local[i, mid:, lanes] = y_low + gain * v[mid:].astype(F32)

    def finish(i, state):
        inter = jnp.dot(c_act[...], state, preferred_element_type=F32)
        grow = jnp.concatenate([jnp.exp(cum_tab[2 * i]), jnp.exp(cum_tab[2 * i + 1])], axis=1)
        out_ref[:, pl.ds(pl.multiple_of(i * PAIR, PAIR), PAIR)] = (
            local[i] + grow * inter
        ).astype(out_ref.dtype)

    def finish_step(j):
        finish(pair_of(own_first, j), ent[j])
        e_copy(j).wait_recv()
        finish(pair_of(other_first, j), e_recv[j])

    most = 2 * steps
    lag = jnp.minimum(steps - 2 + 2 * quad, most)

    @pl.loop(0, most + steps + 2)
    def _(t):
        @pl.when(t == 1)
        def _():
            for r in (1, 2, 3):
                remote(tot.at[0], tot.at[r], tot_sems, r, xor_peer(r)).wait_recv()

        @pl.when((t >= 1) & (t < steps + 1))
        def _():
            t_send[t - 1] = chip_total(2 * t - 2).astype(BF16)
            t_copy(t - 1).start()

        @pl.when(t < steps)
        def _():
            local_states(2 * t)

        @pl.when((t >= 1) & (t < steps + 1))
        def _():
            t_own[t - 1] = chip_total(2 * t - 1)

        @pl.when((t >= lag) & (t < lag + steps))
        def _():
            quad_step(t - lag)

        @pl.when((t >= lag + 1) & (t < lag + 1 + steps))
        def _():
            m = t - lag - 1
            g_copy(m).wait_recv()
            core_step(2 * m, g_recv[m].astype(F32))

        @pl.when(t < steps)
        def _():
            local_states(2 * t + 1)

        @pl.when(t == steps)
        def _():
            raw = jnp.dot(c_act[...], b_t[...], preferred_element_type=F32)
            scores[...] = jnp.where(row_id >= col_id, raw, 0.0)
            cum = cum_cols[...]
            for h in range(heads):
                cum_tab[h] = jnp.broadcast_to(cum[:, h : h + 1], (rows, HEADDIM))

        @pl.when((t >= steps) & (t < 2 * steps))
        def _():
            @pl.loop(0, 2)
            def _(u):
                j = 2 * (t - steps) + u
                intra(pair_of(own_first, j))
                intra(pair_of(other_first, j))

        @pl.when((t >= lag + 2) & (t < lag + 2 + steps))
        def _():
            m = t - lag - 2
            finish_step(2 * m + 1)
            finish_step(2 * m)

    @pl.when(me < n_seq - 1)
    def _():
        halo_copy().wait_send()

    for r in (1, 2, 3):
        remote(tot.at[0], tot.at[r], tot_sems, r, xor_peer(r)).wait_send()

    @pl.loop(0, half)
    def _(j):
        s_copy(j).wait_send()
        e_copy(j).wait_send()

    @pl.loop(0, steps)
    def _(m):
        t_copy(m).wait_send()
        g_copy(m).wait_send()

        @pl.when(has_next)
        def _():
            p_copy(m).wait_send()


def on_device(n_seq, conv_input, conv_weight, step_logit, decay_log, skip_gain):
    taps, channels = conv_weight.shape
    rows = conv_input.shape[0]
    heads = decay_log.shape[0]
    half = heads // 4
    vmem = pl.BlockSpec(memory_space=pltpu.VMEM)
    chunk = (half, STATE, PAIR)
    part = (half // 2, STATE, PAIR)

    def pair_sems(count):
        return pltpu.SemaphoreType.DMA((2, count))

    return pl.pallas_call(
        functools.partial(kernel, n_seq, heads, rows, taps),
        out_shape=jax.ShapeDtypeStruct((rows, heads * HEADDIM), BF16),
        in_specs=[pl.BlockSpec(memory_space=pltpu.HBM)] * 5,
        out_specs=vmem,
        scratch_shapes=[
            pltpu.VMEM((rows, channels), BF16),
            pltpu.VMEM((taps, channels), F32),
            pltpu.VMEM((heads, rows), F32),
            pltpu.VMEM((1, heads), F32),
            pltpu.VMEM((1, heads), F32),
            pltpu.SemaphoreType.DMA((6,)),
            pltpu.VMEM((heads, HEADDIM), F32),
            pltpu.VMEM((8, channels), BF16),
            pltpu.VMEM((2, rows + 8, PAIR), F32),
            pltpu.VMEM((heads // 2, rows, PAIR), BF16),
            pltpu.VMEM((STATE, rows), BF16),
            pltpu.VMEM((rows, STATE), BF16),
            pltpu.VMEM((rows, rows), F32),
            pltpu.VMEM((heads, rows, HEADDIM), F32),
            pltpu.VMEM((heads, rows, HEADDIM), F32),
            pltpu.VMEM((heads, rows), F32),
            pltpu.VMEM((4, heads, HEADDIM), F32),
            pltpu.VMEM((rows, heads), F32),
            pltpu.VMEM((STATE, PAIR), F32),
            pltpu.VMEM(chunk, BF16),
            pltpu.VMEM(chunk, F32),
            pltpu.VMEM(chunk, BF16),
            pltpu.VMEM(part, F32),
            pltpu.VMEM(part, BF16),
            pltpu.VMEM(part, BF16),
            pltpu.VMEM(part, BF16),
            pltpu.VMEM(part, BF16),
            pltpu.VMEM(part, BF16),
            pltpu.VMEM(part, BF16),
            pltpu.VMEM(chunk, BF16),
            pltpu.VMEM(chunk, BF16),
            pltpu.VMEM(chunk, BF16),
            pltpu.VMEM((heads // 2, rows, PAIR), F32),
            pair_sems(1),
            pair_sems(4),
            pair_sems(half),
            pair_sems(half // 2),
            pair_sems(half // 2),
            pair_sems(half // 2),
            pair_sems(half),
        ],
        compiler_params=pltpu.CompilerParams(
            collective_id=0, has_side_effects=True, vmem_limit_bytes=48 * 1024 * 1024
        ),
    )(
        *(
            pltpu.with_memory_space_constraint(operand, pltpu.HBM)
            for operand in (
                conv_input,
                conv_weight,
                step_logit.T,
                decay_log.reshape(1, heads),
                skip_gain.reshape(1, heads),
            )
        )
    )


def solution(mesh):
    return jax.shard_map(
        functools.partial(on_device, mesh.shape["seq"]),
        mesh=mesh,
        in_specs=(P(("grp", "seq"), None), P(), P(("grp", "seq"), None), P(), P()),
        out_specs=P(("grp", "seq"), None),
        check_vma=False,
    )
```
